512 devices in a mesh: section: 32 (over z, x_hi), dp: 4 (over y), mp: 4 (over x_lo, core).
Axes of the slice: x: 4 (x_hi: 2, x_lo: 2; x = x_hi * 2 + x_lo), y: 4, z: 16, core: 2. Of those that a mesh axis runs over, the one named last changes fastest.
Arguments:
- memory: bfloat16 [4, 256, 2048], P('dp', None, ('section', 'mp')), may hold values from -18 to 18
- key_weight: bfloat16 [32, 2048, 2048], P('section', None, 'mp'), may hold values from -1 to 1
- value_weight: bfloat16 [32, 2048, 2048], P('section', None, 'mp'), may hold values from -0.125 to 0.125
- queries: bfloat16 [32, 4, 256, 2048], P('section', 'dp', None, 'mp'), may hold values from -1024 to 1024
- cotangent: bfloat16 [32, 4, 256, 2048], P('section', 'dp', None, 'mp'), may hold values from -6 to 6
- target_lengths: int32 [4], P('dp'), may hold values from 64 to 256, as said below
Outputs:
- context: bfloat16 [32, 4, 256, 2048], P('section', 'dp', None, 'mp')
- mem_grad: float32 [4, 256, 2048], P('dp', None, ('section', 'mp'))
The draws below stay inside these ranges and needn't reach their ends.
Inputs may be any that keep to these rules, and one draw needn't show every extreme that they name: `target_lengths`: valid positions of a sequence come first; the last sequence is full.
All inputs are finite; a program needn't handle non-finite values.
Results may differ from the reference program's by a relative error of at most 0.013.
The reference program's roundings to bfloat16 on the way count: a program that leaves them out, or rounds other values in their place, can miss the bound.
Values may be sent and summed in bfloat16 or wider, within the bound.
No kernel may reach another device: no remote copies, remote signals or barrier semaphores. Data moves between devices by JAX's collectives and lax.ppermute only.
A program may use at most 64 MiB of HBM per device.

```python
import math
import jax
import jax.numpy as jnp
from jax import lax

D = 2048
HEADS = 8
HEAD_DIM = 256
MEM = 256
TGT = 256
LAYERS = 32
SEQS = 4
HW = 2048


def shared_draws(key):
    memory_key = jax.random.fold_in(key, 101)
    weight_key = jax.random.fold_in(key, 102)
    memory = jax.random.truncated_normal(memory_key, -6.0, 6.0, (SEQS, MEM, D), jnp.float32)
    key_weight = jax.random.truncated_normal(weight_key, -4.0, 4.0, (LAYERS, D, HW), jnp.float32) / math.sqrt(D)
    return (memory, key_weight)


def draw_memory(key, part):
    return shared_draws(key)[0].astype(jnp.bfloat16)


def draw_key_weight(key, part):
    return shared_draws(key)[1].astype(jnp.bfloat16)


def draw_queries(key, part):
    base = jax.random.truncated_normal(jax.random.fold_in(key, 104), -6.0, 6.0, (LAYERS, SEQS, TGT, HW), jnp.float32) * 3.0
    return base.astype(jnp.bfloat16)


def draw_target_lengths(key, part):
    jitter = jax.random.randint(jax.random.fold_in(key, 108), (SEQS,), 0, TGT // 4 + 1)
    seq_index = jnp.arange(SEQS)
    rising = TGT // 4 + jitter + TGT // 2 * seq_index // (SEQS - 1)
    return jnp.where(seq_index == SEQS - 1, TGT, jnp.minimum(rising, TGT)).astype(jnp.int32)


def block_scale(key, shape, shards, least, top_value):
    gain = 1.0
    for axis_at, shards_of in shards:
        heights = jax.random.uniform(jax.random.fold_in(jax.random.fold_in(key, 6), axis_at), (shards_of,), jnp.float32, least / len(shards), top_value / len(shards))
        gain = gain * jnp.repeat(jnp.exp(heights), shape[axis_at] // shards_of).reshape((-1,) + (1,) * (len(shape) - 1 - axis_at))
    return gain


def bell_draw(own_key, extent, spread, reach, split=(), kind=jnp.bfloat16):
    values = spread * jax.random.normal(own_key, extent, jnp.float32)
    if split:
        values = values * block_scale(own_key, extent, split, -0.22, 0.18)
    return jnp.clip(values, -reach, reach).astype(kind)


def setup_inputs(seed: int = 0) -> dict:
    seeds = jax.random.split(jax.random.key(seed), 7)
    memory = draw_memory(jax.random.fold_in(seeds[6], 71), 0)
    key_weight = draw_key_weight(jax.random.fold_in(seeds[6], 71), 0)
    value_weight = bell_draw(seeds[2], (LAYERS, D, HW), D ** -0.5, 0.125, ((0, 32), (2, 4)))
    queries = draw_queries(jax.random.fold_in(seeds[6], 71), 0)
    cotangent = bell_draw(seeds[4], (LAYERS, SEQS, TGT, HW), 1.0, 6.0, ((0, 32), (1, 4), (3, 4)))
    target_lengths = draw_target_lengths(jax.random.fold_in(seeds[6], 71), 0)
    return {"memory": memory, "key_weight": key_weight, "value_weight": value_weight, "queries": queries, "cotangent": cotangent, "target_lengths": target_lengths}


def round_low(values_in):
    return lax.optimization_barrier(values_in.astype(jnp.bfloat16)).astype(jnp.float32)


def reference(memory, key_weight, value_weight, queries, cotangent, target_lengths):
    score_scale = HEAD_DIM ** -0.5
    lengths_float = target_lengths.astype(jnp.float32)
    loss_weight = jnp.float32(SEQS * TGT) / jnp.sum(lengths_float)
    valid = (jnp.arange(TGT, dtype=jnp.int32)[None, :] < target_lengths[:, None]).astype(jnp.float32)
    flat_memory = memory.reshape(SEQS * MEM, D)

    def layer_step(running, inputs):
        w_key, w_value, query_rows, cot_rows = inputs
        key_rows = jnp.dot(flat_memory, w_key, preferred_element_type=jnp.float32).astype(jnp.bfloat16)
        value_rows = jnp.dot(flat_memory, w_value, preferred_element_type=jnp.float32).astype(jnp.bfloat16)
        key_heads = key_rows.reshape(SEQS, MEM, HEADS, HEAD_DIM).astype(jnp.float32)
        value_heads = value_rows.reshape(SEQS, MEM, HEADS, HEAD_DIM).astype(jnp.float32)
        query_heads = query_rows.reshape(SEQS, TGT, HEADS, HEAD_DIM).astype(jnp.float32)
        scores = jnp.einsum('bthd,bshd->bhts', query_heads, key_heads) * score_scale
        attention = jax.nn.softmax(scores, axis=-1)
        attention_low = round_low(attention)
        context = jnp.einsum('bhts,bshd->bthd', attention_low, value_heads) * valid[:, :, None, None]
        context = context.astype(jnp.bfloat16)
        weighted = cot_rows.reshape(SEQS, TGT, HEADS, HEAD_DIM).astype(jnp.float32)
        weighted = round_low(weighted * (valid * loss_weight)[:, :, None, None])
        value_grad = jnp.einsum('bhts,bthd->bshd', attention_low, weighted).astype(jnp.bfloat16)
        prob_grad = jnp.einsum('bthd,bshd->bhts', weighted, value_heads)
        row_dot = jnp.sum(attention * prob_grad, axis=-1, keepdims=True)
        score_grad = round_low(attention * (prob_grad - row_dot) * score_scale)
        key_grad = jnp.einsum('bhts,bthd->bshd', score_grad, query_heads).astype(jnp.bfloat16)
        term = jnp.dot(key_grad.reshape(SEQS * MEM, HW), w_key.T, preferred_element_type=jnp.float32)
        term = term + jnp.dot(value_grad.reshape(SEQS * MEM, HW), w_value.T, preferred_element_type=jnp.float32)
        return running + term, context.reshape(SEQS, TGT, HW)

    start_grad = jnp.zeros((SEQS * MEM, D), jnp.float32)
    running, contexts = lax.scan(layer_step, start_grad, (key_weight, value_weight, queries, cotangent))
    return contexts, running.reshape(SEQS, MEM, D)
```

```python
import jax
import jax.numpy as jnp
from jax import lax
from jax.experimental import pallas as pl
from jax.experimental.pallas import tpu as pltpu
from jax.sharding import Mesh, PartitionSpec as P

HEAD_DIM = 256
NT = (((1,), (1,)), ((), ()))
TN = (((0,), (0,)), ((), ()))
X = ("xh", "xl")


def dot(a, b, dims=(((1,), (0,)), ((), ()))):
    return lax.dot_general(a, b, dims, preferred_element_type=jnp.float32)


def local_kernel(
    core_ref, length_ref, own_ref, other_ref, wk_ref, wv_ref, q_ref, cot_ref,
    context_ref, keep_ref, send_ref, mt_ref, m_ref, kg_ref, vg_ref,
):
    core = core_ref[0]
    length = length_ref[0]
    n_x, n_z, blk, rows = own_ref.shape
    span = n_x * blk * 2
    width = wk_ref.shape[1]
    scale = HEAD_DIM ** (-0.5)
    for z in range(n_z):
        for x in range(n_x):
            base = z * span + x * 2 * blk
            mt_ref[pl.ds(pl.multiple_of(base + core * blk, blk), blk), :] = own_ref[x, z]
            mt_ref[pl.ds(pl.multiple_of(base + (1 - core) * blk, blk), blk), :] = other_ref[x, z]
    for z in range(n_z):
        m_ref[:, z * span:(z + 1) * span] = mt_ref[z * span:(z + 1) * span, :].T
    keys = dot(m_ref[...], wk_ref[...]).astype(jnp.bfloat16)
    values = dot(m_ref[...], wv_ref[...]).astype(jnp.bfloat16)
    t_rows = q_ref.shape[0]
    valid = lax.broadcasted_iota(jnp.int32, (t_rows, HEAD_DIM), 0) < length
    for h in range(width // HEAD_DIM):
        cols = slice(h * HEAD_DIM, (h + 1) * HEAD_DIM)
        key, value, query = keys[:, cols], values[:, cols], q_ref[:, cols]
        scores = dot(key, query, NT) * scale
        weights = jnp.exp(scores - jnp.max(scores, axis=0, keepdims=True))
        probs = weights / jnp.sum(weights, axis=0, keepdims=True)
        probs_low = probs.astype(jnp.bfloat16)
        context = dot(probs_low, value, TN)
        context_ref[:, cols] = jnp.where(valid, context, 0.0).astype(jnp.bfloat16)
        cot = jnp.where(valid, cot_ref[:, cols].astype(jnp.float32), 0.0).astype(jnp.bfloat16)
        vg_ref[:, cols] = dot(probs_low, cot).astype(jnp.bfloat16)
        prob_grad = dot(value, cot, NT)
        row_dot = jnp.sum(probs * prob_grad, axis=0, keepdims=True)
        score_grad = (probs * (prob_grad - row_dot) * scale).astype(jnp.bfloat16)
        kg_ref[:, cols] = dot(score_grad, query).astype(jnp.bfloat16)
    first = core == 0
    for z in range(0, n_z, 2):
        at = slice(z * span, (z + 2) * span)
        grad = dot(wk_ref[at, :], kg_ref[...], NT) + dot(wv_ref[at, :], vg_ref[...], NT)
        for dz in range(2):
            for x in range(n_x):
                lo = dz * span + x * 2 * blk
                g0, g1 = grad[lo:lo + blk], grad[lo + blk:lo + 2 * blk]
                keep_ref[x, z + dz] = jnp.where(first, g0, g1).astype(jnp.bfloat16)
                send_ref[x, z + dz] = jnp.where(first, g1, g0).astype(jnp.bfloat16)


def on_device(memory, key_weight, value_weight, queries, cotangent, target_lengths):
    n_z, n_x = lax.axis_size("z"), lax.axis_size("xh") * lax.axis_size("xl")
    rows, blk = memory.shape[1:]
    t_rows, width = queries.shape[2:]
    depth = key_weight.shape[1]
    swap = [(0, 1), (1, 0)]
    n_y = lax.axis_size("y")
    length_tile = jnp.broadcast_to(target_lengths.astype(jnp.float32), (n_y, 8, 128))
    lengths = lax.all_to_all(length_tile, "y", 0, 0)
    loss_weight = float(n_y * t_rows) / jnp.sum(lengths[:, 0, 0])
    mine = memory[0].T
    along_z = lax.all_to_all(jnp.broadcast_to(mine, (n_z, blk, rows)), "z", 0, 0)
    along_z = along_z.reshape(n_z * blk, rows)
    own = lax.all_to_all(jnp.broadcast_to(along_z, (n_x, n_z * blk, rows)), X, 0, 0)
    other = lax.ppermute(own, "c", swap)
    half = (n_x, n_z, blk, rows)
    core = lax.axis_index("c").reshape(1)
    vmem = pl.BlockSpec(memory_space=pltpu.VMEM)
    smem = pl.BlockSpec(memory_space=pltpu.SMEM)
    context, keep, send = pl.pallas_call(
        local_kernel,
        out_shape=(
            jax.ShapeDtypeStruct((t_rows, width), jnp.bfloat16),
            jax.ShapeDtypeStruct(half, jnp.bfloat16),
            jax.ShapeDtypeStruct(half, jnp.bfloat16),
        ),
        in_specs=[smem, smem] + [vmem] * 6,
        out_specs=(vmem, vmem, vmem),
        scratch_shapes=[
            pltpu.VMEM((depth, rows), jnp.bfloat16),
            pltpu.VMEM((rows, depth), jnp.bfloat16),
            pltpu.VMEM((rows, width), jnp.bfloat16),
            pltpu.VMEM((rows, width), jnp.bfloat16),
        ],
        compiler_params=pltpu.CompilerParams(vmem_limit_bytes=24 << 20),
        cost_estimate=pl.CostEstimate(flops=2500000000, bytes_accessed=8 << 20, transcendentals=1 << 17),
    )(
        core, target_lengths, own.reshape(half), other.reshape(half),
        key_weight[0], value_weight[0], queries[0, 0], cotangent[0, 0],
    )
    got = lax.ppermute(send, "c", swap)
    pair = (keep.astype(jnp.float32) + got.astype(jnp.float32)).astype(jnp.bfloat16)
    parts = lax.all_to_all(pair.reshape(n_x, n_z * blk, rows), X, 0, 0)
    row_sum = jnp.sum(parts.astype(jnp.float32), axis=0).astype(jnp.bfloat16)
    parts = lax.all_to_all(row_sum.reshape(n_z, blk, rows), "z", 0, 0)
    own_grad = jnp.sum(parts.astype(jnp.float32), axis=0) * loss_weight
    return context[None, None], own_grad.T[None]


def solution(mesh):
    fine = Mesh(mesh.devices.reshape(16, 2, 4, 2, 2), ("z", "xh", "y", "xl", "c"))
    layers, heads, features = ("z", "xh"), ("xl", "c"), ("z", "xh", "xl", "c")
    return jax.shard_map(
        on_device,
        mesh=fine,
        in_specs=(
            P("y", None, features),
            P(layers, None, heads),
            P(layers, None, heads),
            P(layers, "y", None, heads),
            P(layers, "y", None, heads),
            P("y"),
        ),
        out_specs=(P(layers, "y", None, heads), P("y", None, features)),
        check_vma=False,
    )
```

```python
import jax
import jax.numpy as jnp
from jax import lax
from jax.experimental import pallas as pl
from jax.experimental.pallas import tpu as pltpu
from jax.sharding import Mesh, PartitionSpec as P


HEAD_DIM = 256
NT = (((1,), (1,)), ((), ()))
TN = (((0,), (0,)), ((), ()))
X = ("xh", "xl")


def dot(a, b, dims=(((1,), (0,)), ((), ()))):
    return lax.dot_general(a, b, dims, preferred_element_type=jnp.float32)


def local_kernel(
    core_ref, length_ref, own_ref, other_ref, wk_ref, wv_hbm, q_hbm, cot_hbm,
    context_ref, keep_ref, send_ref,
    mt_ref, m_ref, kg_ref, vg_ref, wv_ref, q_ref, cot_ref, sems,
):
    loads = [
        pltpu.make_async_copy(src, dst, sems.at[i])
        for i, (src, dst) in enumerate(((q_hbm, q_ref), (wv_hbm, wv_ref), (cot_hbm, cot_ref)))
    ]
    for load in loads:
        load.start()
    core = core_ref[0]
    length = length_ref[0]
    n_x, n_z, blk, _ = own_ref.shape
    span = n_x * blk * 2
    width = wk_ref.shape[1]
    scale = HEAD_DIM ** (-0.5)
    for z in range(n_z):
        for x in range(n_x):
            base = z * span + x * 2 * blk
            mt_ref[pl.ds(pl.multiple_of(base + core * blk, blk), blk), :] = own_ref[x, z]
            mt_ref[pl.ds(pl.multiple_of(base + (1 - core) * blk, blk), blk), :] = other_ref[x, z]
    for z in range(n_z):
        m_ref[:, z * span:(z + 1) * span] = mt_ref[z * span:(z + 1) * span, :].T
    keys = dot(m_ref[...], wk_ref[...]).astype(jnp.bfloat16)
    t_rows = q_ref.shape[0]
    valid = lax.broadcasted_iota(jnp.int32, (t_rows, HEAD_DIM), 0) < length
    heads = [slice(h, h + HEAD_DIM) for h in range(0, width, HEAD_DIM)]
    loads[0].wait()
    all_probs = []
    for cols in heads:
        scores = dot(keys[:, cols], q_ref[:, cols], NT) * scale
        weights = jnp.exp(scores - jnp.max(scores, axis=0, keepdims=True))
        all_probs.append(weights / jnp.sum(weights, axis=0, keepdims=True))
    loads[1].wait()
    values = dot(m_ref[...], wv_ref[...]).astype(jnp.bfloat16)
    loads[2].wait()
    for cols, probs in zip(heads, all_probs):
        value = values[:, cols]
        probs_low = probs.astype(jnp.bfloat16)
        context = dot(probs_low, value, TN)
        context_ref[:, cols] = jnp.where(valid, context, 0.0).astype(jnp.bfloat16)
        cot = jnp.where(valid, cot_ref[:, cols].astype(jnp.float32), 0.0).astype(jnp.bfloat16)
        vg_ref[:, cols] = dot(probs_low, cot).astype(jnp.bfloat16)
        prob_grad = dot(value, cot, NT)
        row_dot = jnp.sum(probs * prob_grad, axis=0, keepdims=True)
        score_grad = (probs * (prob_grad - row_dot) * scale).astype(jnp.bfloat16)
        kg_ref[:, cols] = dot(score_grad, q_ref[:, cols]).astype(jnp.bfloat16)
    first = core == 0
    for z in range(0, n_z, 2):
        at = slice(z * span, (z + 2) * span)
        grad = dot(wk_ref[at, :], kg_ref[...], NT) + dot(wv_ref[at, :], vg_ref[...], NT)
        for dz in range(2):
            for x in range(n_x):
                lo = dz * span + x * 2 * blk
                g0, g1 = grad[lo:lo + blk], grad[lo + blk:lo + 2 * blk]
                keep_ref[x, z + dz] = jnp.where(first, g0, g1).astype(jnp.bfloat16)
                send_ref[x, z + dz] = jnp.where(first, g1, g0).astype(jnp.bfloat16)


def on_device(memory, key_weight, value_weight, queries, cotangent, target_lengths):
    n_z, n_x = lax.axis_size("z"), lax.axis_size("xh") * lax.axis_size("xl")
    rows, blk = memory.shape[1:]
    t_rows, width = queries.shape[2:]
    depth = key_weight.shape[1]
    swap = [(0, 1), (1, 0)]
    n_y = lax.axis_size("y")
    tokens = jnp.broadcast_to(target_lengths.astype(jnp.float32), (8, 128))
    tokens = tokens + lax.ppermute(tokens, "y", [(y, y ^ 1) for y in range(n_y)])
    mine = memory[0].T
    to_z = jnp.broadcast_to(mine, (n_z, blk, rows))
    along_z = lax.all_to_all(to_z, "z", 0, 0)
    along_z, tokens = lax.optimization_barrier((along_z, tokens))
    along_z = along_z.reshape(n_z * blk, rows)
    own = lax.all_to_all(jnp.broadcast_to(along_z, (n_x, n_z * blk, rows)), X, 0, 0)
    other = lax.ppermute(own, "c", swap)
    half = (n_x, n_z, blk, rows)
    core = lax.axis_index("c").reshape(1)
    vmem = pl.BlockSpec(memory_space=pltpu.VMEM)
    smem = pl.BlockSpec(memory_space=pltpu.SMEM)
    context, keep, send = pl.pallas_call(
        local_kernel,
        out_shape=(
            jax.ShapeDtypeStruct((t_rows, width), jnp.bfloat16),
            jax.ShapeDtypeStruct(half, jnp.bfloat16),
            jax.ShapeDtypeStruct(half, jnp.bfloat16),
        ),
        in_specs=[smem, smem] + [vmem] * 3 + [pl.BlockSpec(memory_space=pltpu.HBM)] * 3,
        out_specs=(vmem, vmem, vmem),
        scratch_shapes=[
            pltpu.VMEM((depth, rows), jnp.bfloat16),
            pltpu.VMEM((rows, depth), jnp.bfloat16),
            pltpu.VMEM((rows, width), jnp.bfloat16),
            pltpu.VMEM((rows, width), jnp.bfloat16),
            pltpu.VMEM((depth, width), jnp.bfloat16),
            pltpu.VMEM((t_rows, width), jnp.bfloat16),
            pltpu.VMEM((t_rows, width), jnp.bfloat16),
            pltpu.SemaphoreType.DMA((3,)),
        ],
        compiler_params=pltpu.CompilerParams(vmem_limit_bytes=24 << 20),
        cost_estimate=pl.CostEstimate(flops=2500000000, bytes_accessed=8 << 20, transcendentals=1 << 17),
    )(
        core, target_lengths, own.reshape(half), other.reshape(half),
        key_weight[0], *[pltpu.with_memory_space_constraint(a, pltpu.HBM) for a in (value_weight[0], queries[0, 0], cotangent[0, 0])],
    )
    got = lax.ppermute(send, "c", swap)
    pair = (keep.astype(jnp.float32) + got.astype(jnp.float32)).astype(jnp.bfloat16)
    parts = lax.all_to_all(pair.reshape(n_x, n_z * blk, rows), X, 0, 0)
    row_sum = jnp.sum(parts.astype(jnp.float32), axis=0).astype(jnp.bfloat16)
    parts = lax.all_to_all(row_sum.reshape(n_z, blk, rows), "z", 0, 0)
    tokens = tokens + lax.ppermute(tokens, "y", [(y, y ^ 2) for y in range(n_y)])
    loss_weight = float(n_y * t_rows) / tokens[0, 0]
    own_grad = jnp.sum(parts.astype(jnp.float32), axis=0) * loss_weight
    return context[None, None], own_grad.T[None]


def solution(mesh):
    fine = Mesh(mesh.devices.reshape(16, 2, 4, 2, 2), ("z", "xh", "y", "xl", "c"))
    layers, heads, features = ("z", "xh"), ("xl", "c"), ("z", "xh", "xl", "c")
    return jax.shard_map(
        on_device,
        mesh=fine,
        in_specs=(
            P("y", None, features),
            P(layers, None, heads),
            P(layers, None, heads),
            P(layers, "y", None, heads),
            P(layers, "y", None, heads),
            P("y"),
        ),
        out_specs=(P(layers, "y", None, heads), P("y", None, features)),
        check_vma=False,
    )
```

```python
import functools

import jax
import jax.numpy as jnp
from jax import lax
from jax.experimental import pallas as pl
from jax.experimental.pallas import tpu as pltpu
from jax.sharding import Mesh, PartitionSpec as P

HEAD_DIM = 256
NN = (((1,), (0,)), ((), ()))
NT = (((1,), (1,)), ((), ()))
TN = (((0,), (0,)), ((), ()))
X = ("xh", "xl")


def dot(a, b, dims=NN):
    return lax.dot_general(a, b, dims, preferred_element_type=jnp.float32)


def from_member(n, first):
    return [(first + i) % n for i in range(n)]


def feature_rows(ref, x, core, shape, order):
    n_x, _, blk, _ = shape
    return jnp.concatenate(
        [
            ref[pl.ds(pl.multiple_of((z * n_x + x) * 2 * blk + core * blk, blk), blk), :]
            for z in order
        ],
        axis=0,
    )


def own_kernel(
    order, core_ref, own_ref, wk_ref, wv_hbm, q_hbm, cot_hbm,
    wv_ref, q_ref, cot_ref, m_ref, key_part_ref, sems,
):
    loads = [
        pltpu.make_async_copy(src, dst, sems.at[i])
        for i, (src, dst) in enumerate(((wv_hbm, wv_ref), (q_hbm, q_ref), (cot_hbm, cot_ref)))
    ]
    for load in loads:
        load.start()
    n_x, n_z, blk, rows = own_ref.shape
    core = core_ref[0]
    total = None
    for x in range(n_x):
        mem = own_ref[x].reshape(n_z * blk, rows).T
        m_ref[:, x * n_z * blk:(x + 1) * n_z * blk] = mem
        part = dot(mem, feature_rows(wk_ref, x, core, own_ref.shape, order))
        total = part if total is None else total + part
    key_part_ref[...] = total
    for load in loads:
        load.wait()


def main_kernel(
    order, sum_order, core_ref, length_ref, other_ref, own_m_ref, key_part_ref, wk_ref, wv_ref, q_ref, cot_ref,
    context_hbm, send_ref, kg_ref, vg_ref, context_ref, sem,
):
    n_x, n_z, blk, rows = other_ref.shape
    core = core_ref[0]
    width = wk_ref.shape[1]
    scale = HEAD_DIM ** (-0.5)
    keys, values = key_part_ref[...], None
    for x in range(n_x):
        mem = other_ref[x].reshape(n_z * blk, rows).T
        keys = keys + dot(mem, feature_rows(wk_ref, x, 1 - core, other_ref.shape, order))
        part = dot(mem, feature_rows(wv_ref, x, 1 - core, other_ref.shape, order))
        values = part if values is None else values + part
        own = own_m_ref[:, x * n_z * blk:(x + 1) * n_z * blk]
        values = values + dot(own, feature_rows(wv_ref, x, core, other_ref.shape, order))
    keys, values = keys.astype(jnp.bfloat16), values.astype(jnp.bfloat16)
    t_rows = q_ref.shape[0]
    row = lax.broadcasted_iota(jnp.int32, (t_rows, HEAD_DIM), 0)
    valid = row.astype(jnp.float32) < length_ref[0:1, 0:1]
    heads = [slice(h, h + HEAD_DIM) for h in range(0, width, HEAD_DIM)]
    kept = []
    for cols in heads:
        scores = dot(keys[:, cols], q_ref[:, cols], NT) * scale
        weights = jnp.exp(scores - jnp.max(scores, axis=0, keepdims=True))
        probs = weights * (1.0 / jnp.sum(weights, axis=0, keepdims=True))
        probs_low = probs.astype(jnp.bfloat16)
        context = dot(probs_low, values[:, cols], TN)
        context_ref[:, cols] = jnp.where(valid, context, 0.0).astype(jnp.bfloat16)
        kept.append((probs, probs_low))
    out = pltpu.make_async_copy(context_ref, context_hbm, sem)
    out.start()
    for cols, (probs, probs_low) in zip(heads, kept):
        cot = jnp.where(valid, cot_ref[:, cols].astype(jnp.float32), 0.0).astype(jnp.bfloat16)
        vg_ref[:, cols] = dot(probs_low, cot).astype(jnp.bfloat16)
        prob_grad = dot(values[:, cols], cot, NT)
        row_dot = jnp.sum(probs * prob_grad, axis=0, keepdims=True)
        score_grad = (probs * (prob_grad - row_dot) * scale).astype(jnp.bfloat16)
        kg_ref[:, cols] = dot(score_grad, q_ref[:, cols]).astype(jnp.bfloat16)
    half_grad(sum_order, 1 - core, wk_ref, wv_ref, kg_ref, vg_ref, send_ref)
    out.wait()


def half_grad(order, core, wk_ref, wv_ref, kg_ref, vg_ref, out_ref):
    n_x, n_z, blk, rows = out_ref.shape
    kg, vg = kg_ref[...], vg_ref[...]
    for x in range(n_x):
        grad = dot(feature_rows(wk_ref, x, core, out_ref.shape, order), kg, NT)
        grad = grad + dot(feature_rows(wv_ref, x, core, out_ref.shape, order), vg, NT)
        out_ref[x] = grad.astype(jnp.bfloat16).reshape(n_z, blk, rows)


def keep_kernel(order, core_ref, wk_ref, wv_ref, kg_ref, vg_ref, keep_ref):
    half_grad(order, core_ref[0], wk_ref, wv_ref, kg_ref, vg_ref, keep_ref)


def on_device(memory, key_weight, value_weight, queries, cotangent, target_lengths):
    n_z, n_x = lax.axis_size("z"), lax.axis_size("xh") * lax.axis_size("xl")
    rows, blk = memory.shape[1:]
    t_rows, width = queries.shape[2:]
    depth = key_weight.shape[1]
    n_y = lax.axis_size("y")
    swap = [(0, 1), (1, 0)]
    half = (n_x, n_z, blk, rows)
    core = lax.axis_index("c").reshape(1)
    w_key = key_weight[0]
    w_value, query, cot = (
        pltpu.with_memory_space_constraint(a, pltpu.HBM)
        for a in (value_weight[0], queries[0, 0], cotangent[0, 0])
    )
    vmem = pl.BlockSpec(memory_space=pltpu.VMEM)
    smem = pl.BlockSpec(memory_space=pltpu.SMEM)
    hbm = pl.BlockSpec(memory_space=pltpu.HBM)
    params = pltpu.CompilerParams(vmem_limit_bytes=16 << 20)

    def low(*shape):
        return jax.ShapeDtypeStruct(shape, jnp.bfloat16)

    order = sum_order = from_member(n_z, n_z // 2)
    to_z = jnp.broadcast_to(memory[0].T, (n_z, blk, rows))
    along_z = lax.all_to_all(to_z, "z", 0, 0, axis_index_groups=[order])
    length = jnp.broadcast_to(target_lengths.astype(jnp.float32), (blk, rows))
    tokens = length + lax.ppermute(length, "y", [(y, y ^ 1) for y in range(n_y)])
    along_z, tokens = lax.optimization_barrier((along_z, tokens))
    along_z = along_z.reshape(n_z * blk, rows)
    to_x = jnp.broadcast_to(along_z, (n_x, n_z * blk, rows))
    own = lax.all_to_all(to_x, X, 0, 0)
    tokens = tokens + lax.ppermute(tokens, "y", [(y, y ^ 2) for y in range(n_y)])
    own, loss_weight = lax.optimization_barrier((own, float(n_y * t_rows) / tokens))
    other = lax.ppermute(own, "c", swap).reshape(half)
    w_value, query, cot, own_m, key_part = pl.pallas_call(
        functools.partial(own_kernel, order),
        out_shape=(
            low(depth, width), low(t_rows, width), low(t_rows, width), low(rows, depth // 2),
            jax.ShapeDtypeStruct((rows, width), jnp.float32),
        ),
        in_specs=[smem, vmem, vmem, hbm, hbm, hbm],
        out_specs=(vmem,) * 5,
        scratch_shapes=[pltpu.SemaphoreType.DMA((3,))],
        compiler_params=params,
        cost_estimate=pl.CostEstimate(flops=270000000, bytes_accessed=8 << 20, transcendentals=0),
    )(core, own.reshape(half), w_key, w_value, query, cot)
    context, send, key_grad, value_grad = pl.pallas_call(
        functools.partial(main_kernel, order, sum_order),
        out_shape=(low(t_rows, width), low(*half), low(rows, width), low(rows, width)),
        in_specs=[smem] + [vmem] * 8,
        out_specs=(hbm, vmem, vmem, vmem),
        scratch_shapes=[
            pltpu.VMEM((t_rows, width), jnp.bfloat16),
            pltpu.SemaphoreType.DMA,
        ],
        compiler_params=params,
        cost_estimate=pl.CostEstimate(flops=1700000000, bytes_accessed=8 << 20, transcendentals=1 << 17),
    )(core, length, other, own_m, key_part, w_key, w_value, query, cot)
    got = lax.ppermute(send, "c", swap)
    keep = pl.pallas_call(
        functools.partial(keep_kernel, sum_order),
        out_shape=low(*half),
        in_specs=[smem] + [vmem] * 4,
        out_specs=vmem,
        compiler_params=params,
        cost_estimate=pl.CostEstimate(flops=540000000, bytes_accessed=5 << 20, transcendentals=0),
    )(core, w_key, w_value, key_grad, value_grad)
    pair = (keep.astype(jnp.float32) + got.astype(jnp.float32)).astype(jnp.bfloat16)
    parts = lax.all_to_all(pair.reshape(n_x, n_z * blk, rows), X, 0, 0)
    row_sum = jnp.sum(parts.astype(jnp.float32), axis=0).astype(jnp.bfloat16)
    parts = lax.all_to_all(row_sum.reshape(n_z, blk, rows), "z", 0, 0, axis_index_groups=[sum_order])
    own_grad = jnp.sum(parts.astype(jnp.float32), axis=0) * loss_weight
    return context[None, None], own_grad.T[None]


def solution(mesh):
    fine = Mesh(mesh.devices.reshape(16, 2, 4, 2, 2), ("z", "xh", "y", "xl", "c"))
    layers, heads, features = ("z", "xh"), ("xl", "c"), ("z", "xh", "xl", "c")
    return jax.shard_map(
        on_device,
        mesh=fine,
        in_specs=(
            P("y", None, features),
            P(layers, None, heads),
            P(layers, None, heads),
            P(layers, "y", None, heads),
            P(layers, "y", None, heads),
            P("y"),
        ),
        out_specs=(P(layers, "y", None, heads), P("y", None, features)),
        check_vma=False,
    )
```

```python
import functools

import jax
import jax.numpy as jnp
from jax import lax
from jax.experimental import pallas as pl
from jax.experimental.pallas import tpu as pltpu
from jax.sharding import Mesh, PartitionSpec as P

HEAD_DIM = 256
NN = (((1,), (0,)), ((), ()))
NT = (((1,), (1,)), ((), ()))
TN = (((0,), (0,)), ((), ()))
X = ("xh", "xl")


def dot(a, b, dims=NN):
    return lax.dot_general(a, b, dims, preferred_element_type=jnp.float32)


def from_member(n, first):
    return [(first + i) % n for i in range(n)]


def feature_rows(ref, x, core, shape, order):
    n_x, _, blk, _ = shape
    z_order, x_order = order
    at = x_order[x]
    return jnp.concatenate(
        [
            ref[pl.ds(pl.multiple_of((z * n_x + at) * 2 * blk + core * blk, blk), blk), :]
            for z in z_order
        ],
        axis=0,
    )


def own_kernel(
    order, core_ref, own_ref, wk_ref, wv_hbm, q_hbm, cot_hbm,
    wv_ref, q_ref, cot_ref, m_ref, key_part_ref, sems,
):
    loads = [
        pltpu.make_async_copy(src, dst, sems.at[i])
        for i, (src, dst) in enumerate(((wv_hbm, wv_ref), (q_hbm, q_ref), (cot_hbm, cot_ref)))
    ]
    for load in loads:
        load.start()
    n_x, n_z, blk, rows = own_ref.shape
    core = core_ref[0]
    total = None
    for x in range(n_x):
        mem = own_ref[x].reshape(n_z * blk, rows).T
        m_ref[:, x * n_z * blk:(x + 1) * n_z * blk] = mem
        part = dot(mem, feature_rows(wk_ref, x, core, own_ref.shape, order))
        total = part if total is None else total + part
    key_part_ref[...] = total
    for load in loads:
        load.wait()


def main_kernel(
    order, sum_order, core_ref, length_ref, other_ref, own_m_ref, key_part_ref, wk_ref, wv_ref, q_ref, cot_ref,
    context_hbm, send_ref, kg_ref, vg_ref, context_ref, sem,
):
    n_x, n_z, blk, rows = other_ref.shape
    core = core_ref[0]
    width = wk_ref.shape[1]
    scale = HEAD_DIM ** (-0.5)
    keys, values = key_part_ref[...], None
    for x in range(n_x):
        mem = other_ref[x].reshape(n_z * blk, rows).T
        keys = keys + dot(mem, feature_rows(wk_ref, x, 1 - core, other_ref.shape, order))
        part = dot(mem, feature_rows(wv_ref, x, 1 - core, other_ref.shape, order))
        values = part if values is None else values + part
        own = own_m_ref[:, x * n_z * blk:(x + 1) * n_z * blk]
        values = values + dot(own, feature_rows(wv_ref, x, core, other_ref.shape, order))
    keys, values = keys.astype(jnp.bfloat16), values.astype(jnp.bfloat16)
    t_rows = q_ref.shape[0]
    row = lax.broadcasted_iota(jnp.int32, (t_rows, HEAD_DIM), 0)
    valid = row.astype(jnp.float32) < length_ref[0:1, 0:1]
    heads = [slice(h, h + HEAD_DIM) for h in range(0, width, HEAD_DIM)]
    kept = []
    for cols in heads:
        scores = dot(keys[:, cols], q_ref[:, cols], NT) * scale
        weights = jnp.exp(scores - jnp.max(scores, axis=0, keepdims=True))
        probs = weights * (1.0 / jnp.sum(weights, axis=0, keepdims=True))
        probs_low = probs.astype(jnp.bfloat16)
        context = dot(probs_low, values[:, cols], TN)
        context_ref[:, cols] = jnp.where(valid, context, 0.0).astype(jnp.bfloat16)
        kept.append((probs, probs_low))
    out = pltpu.make_async_copy(context_ref, context_hbm, sem)
    out.start()
    for cols, (probs, probs_low) in zip(heads, kept):
        cot = jnp.where(valid, cot_ref[:, cols].astype(jnp.float32), 0.0).astype(jnp.bfloat16)
        vg_ref[:, cols] = dot(probs_low, cot).astype(jnp.bfloat16)
        prob_grad = dot(values[:, cols], cot, NT)
        row_dot = jnp.sum(probs * prob_grad, axis=0, keepdims=True)
        score_grad = (probs * (prob_grad - row_dot) * scale).astype(jnp.bfloat16)
        kg_ref[:, cols] = dot(score_grad, q_ref[:, cols]).astype(jnp.bfloat16)
    half_grad(sum_order, 1 - core, wk_ref, wv_ref, kg_ref, vg_ref, send_ref)
    out.wait()


def half_grad(order, core, wk_ref, wv_ref, kg_ref, vg_ref, out_ref):
    n_x, n_z, blk, rows = out_ref.shape
    kg, vg = kg_ref[...], vg_ref[...]
    for x in range(n_x):
        grad = dot(feature_rows(wk_ref, x, core, out_ref.shape, order), kg, NT)
        grad = grad + dot(feature_rows(wv_ref, x, core, out_ref.shape, order), vg, NT)
        out_ref[x] = grad.astype(jnp.bfloat16).reshape(n_z, blk, rows)


def keep_kernel(order, core_ref, wk_ref, wv_ref, kg_ref, vg_ref, keep_ref):
    half_grad(order, core_ref[0], wk_ref, wv_ref, kg_ref, vg_ref, keep_ref)


def on_device(memory, key_weight, value_weight, queries, cotangent, target_lengths):
    n_z, n_x = lax.axis_size("z"), lax.axis_size("xh") * lax.axis_size("xl")
    rows, blk = memory.shape[1:]
    t_rows, width = queries.shape[2:]
    depth = key_weight.shape[1]
    n_y = lax.axis_size("y")
    swap = [(0, 1), (1, 0)]
    half = (n_x, n_z, blk, rows)
    core = lax.axis_index("c").reshape(1)
    w_key = key_weight[0]
    w_value, query, cot = (
        pltpu.with_memory_space_constraint(a, pltpu.HBM)
        for a in (value_weight[0], queries[0, 0], cotangent[0, 0])
    )
    vmem = pl.BlockSpec(memory_space=pltpu.VMEM)
    smem = pl.BlockSpec(memory_space=pltpu.SMEM)
    hbm = pl.BlockSpec(memory_space=pltpu.HBM)
    params = pltpu.CompilerParams(vmem_limit_bytes=16 << 20)

    def low(*shape):
        return jax.ShapeDtypeStruct(shape, jnp.bfloat16)

    order = from_member(n_z, n_z * 11 // 16), from_member(n_x, 0)
    sum_order = from_member(n_z, n_z // 2), from_member(n_x, n_x // 2)
    to_z = jnp.broadcast_to(memory[0].T, (n_z, blk, rows))
    along_z = lax.all_to_all(to_z, "z", 0, 0, axis_index_groups=[order[0]])
    length = jnp.broadcast_to(target_lengths.astype(jnp.float32), (blk, rows))
    tokens = length + lax.ppermute(length, "y", [(y, y ^ 1) for y in range(n_y)])
    along_z, tokens = lax.optimization_barrier((along_z, tokens))
    along_z = along_z.reshape(n_z * blk, rows)
    to_x = jnp.broadcast_to(along_z, (n_x, n_z * blk, rows))
    own = lax.all_to_all(to_x, X, 0, 0, axis_index_groups=[order[1]])
    tokens = tokens + lax.ppermute(tokens, "y", [(y, n_y - 1 - y) for y in range(n_y)])
    own, loss_weight = lax.optimization_barrier((own, float(n_y * t_rows) / tokens))
    other = lax.ppermute(own, "c", swap).reshape(half)
    w_value, query, cot, own_m, key_part = pl.pallas_call(
        functools.partial(own_kernel, order),
        out_shape=(
            low(depth, width), low(t_rows, width), low(t_rows, width), low(rows, depth // 2),
            jax.ShapeDtypeStruct((rows, width), jnp.float32),
        ),
        in_specs=[smem, vmem, vmem, hbm, hbm, hbm],
        out_specs=(vmem,) * 5,
        scratch_shapes=[pltpu.SemaphoreType.DMA((3,))],
        compiler_params=params,
        cost_estimate=pl.CostEstimate(flops=270000000, bytes_accessed=8 << 20, transcendentals=0),
    )(core, own.reshape(half), w_key, w_value, query, cot)
    context, send, key_grad, value_grad = pl.pallas_call(
        functools.partial(main_kernel, order, sum_order),
        out_shape=(low(t_rows, width), low(*half), low(rows, width), low(rows, width)),
        in_specs=[smem] + [vmem] * 8,
        out_specs=(hbm, vmem, vmem, vmem),
        scratch_shapes=[
            pltpu.VMEM((t_rows, width), jnp.bfloat16),
            pltpu.SemaphoreType.DMA,
        ],
        compiler_params=params,
        cost_estimate=pl.CostEstimate(flops=1700000000, bytes_accessed=8 << 20, transcendentals=1 << 17),
    )(core, length, other, own_m, key_part, w_key, w_value, query, cot)
    got = lax.ppermute(send, "c", swap)
    keep = pl.pallas_call(
        functools.partial(keep_kernel, sum_order),
        out_shape=low(*half),
        in_specs=[smem] + [vmem] * 4,
        out_specs=vmem,
        compiler_params=params,
        cost_estimate=pl.CostEstimate(flops=540000000, bytes_accessed=5 << 20, transcendentals=0),
    )(core, w_key, w_value, key_grad, value_grad)
    pair = (keep.astype(jnp.float32) + got.astype(jnp.float32)).astype(jnp.bfloat16)
    parts = lax.all_to_all(
        pair.reshape(n_x, n_z * blk, rows), X, 0, 0, axis_index_groups=[sum_order[1]]
    )
    row_sum = jnp.sum(parts.astype(jnp.float32), axis=0).astype(jnp.bfloat16)
    parts = lax.all_to_all(row_sum.reshape(n_z, blk, rows), "z", 0, 0, axis_index_groups=[sum_order[0]])
    own_grad = jnp.sum(parts.astype(jnp.float32), axis=0) * loss_weight
    return context[None, None], own_grad.T[None]


def solution(mesh):
    fine = Mesh(mesh.devices.reshape(16, 2, 4, 2, 2), ("z", "xh", "y", "xl", "c"))
    layers, heads, features = ("z", "xh"), ("xl", "c"), ("z", "xh", "xl", "c")
    return jax.shard_map(
        on_device,
        mesh=fine,
        in_specs=(
            P("y", None, features),
            P(layers, None, heads),
            P(layers, None, heads),
            P(layers, "y", None, heads),
            P(layers, "y", None, heads),
            P("y"),
        ),
        out_specs=(P(layers, "y", None, heads), P("y", None, features)),
        check_vma=False,
    )
```

```python
import functools

import jax
import jax.numpy as jnp
from jax import lax
from jax.experimental import pallas as pl
from jax.experimental.pallas import tpu as pltpu
from jax.sharding import Mesh, PartitionSpec as P

HEAD_DIM = 256
NN = (((1,), (0,)), ((), ()))
NT = (((1,), (1,)), ((), ()))
TN = (((0,), (0,)), ((), ()))
X = ("xh", "xl")


def dot(a, b, dims=NN):
    return lax.dot_general(a, b, dims, preferred_element_type=jnp.float32)


def from_member(n, first):
    return [(first + i) % n for i in range(n)]


def feature_rows(ref, x, core, shape, order):
    n_x, _, blk, _ = shape
    z_order, x_order = order
    at = x_order[x]
    return jnp.concatenate(
        [
            ref[pl.ds(pl.multiple_of((z * n_x + at) * 2 * blk + core * blk, blk), blk), :]
            for z in z_order
        ],
        axis=0,
    )


def own_kernel(
    order, core_ref, own_ref, wk_ref, wv_hbm, q_hbm, cot_hbm,
    wv_ref, q_ref, cot_ref, m_ref, key_part_ref, sems,
):
    loads = [
        pltpu.make_async_copy(src, dst, sems.at[i])
        for i, (src, dst) in enumerate(((wv_hbm, wv_ref), (q_hbm, q_ref), (cot_hbm, cot_ref)))
    ]
    for load in loads:
        load.start()
    n_x, n_z, blk, rows = own_ref.shape
    core = core_ref[0]
    total = None
    for x in range(n_x):
        mem = own_ref[x].reshape(n_z * blk, rows).T
        m_ref[:, x * n_z * blk:(x + 1) * n_z * blk] = mem
        part = dot(mem, feature_rows(wk_ref, x, core, own_ref.shape, order))
        total = part if total is None else total + part
    key_part_ref[...] = total
    for load in loads:
        load.wait()


def main_kernel(
    order, sum_order, core_ref, length_ref, other_ref, own_m_ref, key_part_ref, wk_ref, wv_ref, q_ref, cot_ref,
    send_ref, kg_ref, vg_ref, probs_ref, values_ref,
):
    n_x, n_z, blk, rows = other_ref.shape
    core = core_ref[0]
    width = wk_ref.shape[1]
    scale = HEAD_DIM ** (-0.5)
    keys, values = key_part_ref[...], None
    for x in range(n_x):
        mem = other_ref[x].reshape(n_z * blk, rows).T
        keys = keys + dot(mem, feature_rows(wk_ref, x, 1 - core, other_ref.shape, order))
        part = dot(mem, feature_rows(wv_ref, x, 1 - core, other_ref.shape, order))
        values = part if values is None else values + part
        own = own_m_ref[:, x * n_z * blk:(x + 1) * n_z * blk]
        values = values + dot(own, feature_rows(wv_ref, x, core, other_ref.shape, order))
    keys, values = keys.astype(jnp.bfloat16), values.astype(jnp.bfloat16)
    t_rows = q_ref.shape[0]
    row = lax.broadcasted_iota(jnp.int32, (t_rows, HEAD_DIM), 0)
    valid = row.astype(jnp.float32) < length_ref[0:1, 0:1]
    heads = [slice(h, h + HEAD_DIM) for h in range(0, width, HEAD_DIM)]
    kept = []
    for cols in heads:
        scores = dot(keys[:, cols], q_ref[:, cols], NT) * scale
        weights = jnp.exp(scores - jnp.max(scores, axis=0, keepdims=True))
        probs = weights * (1.0 / jnp.sum(weights, axis=0, keepdims=True))
        probs_low = probs.astype(jnp.bfloat16)
        probs_ref[:, len(kept) * t_rows:(len(kept) + 1) * t_rows] = probs_low
        kept.append((probs, probs_low))
    values_ref[...] = values
    for cols, (probs, probs_low) in zip(heads, kept):
        cot = jnp.where(valid, cot_ref[:, cols].astype(jnp.float32), 0.0).astype(jnp.bfloat16)
        vg_ref[:, cols] = dot(probs_low, cot).astype(jnp.bfloat16)
        prob_grad = dot(values[:, cols], cot, NT)
        row_dot = jnp.sum(probs * prob_grad, axis=0, keepdims=True)
        score_grad = (probs * (prob_grad - row_dot) * scale).astype(jnp.bfloat16)
        kg_ref[:, cols] = dot(score_grad, q_ref[:, cols]).astype(jnp.bfloat16)
    half_grad(sum_order, 1 - core, wk_ref, wv_ref, kg_ref, vg_ref, send_ref)


def half_grad(order, core, wk_ref, wv_ref, kg_ref, vg_ref, out_ref):
    n_x, n_z, blk, rows = out_ref.shape
    kg, vg = kg_ref[...], vg_ref[...]
    for x in range(n_x):
        grad = dot(feature_rows(wk_ref, x, core, out_ref.shape, order), kg, NT)
        grad = grad + dot(feature_rows(wv_ref, x, core, out_ref.shape, order), vg, NT)
        out_ref[x] = grad.astype(jnp.bfloat16).reshape(n_z, blk, rows)


def keep_kernel(
    order, core_ref, length_ref, wk_ref, wv_ref, kg_ref, vg_ref, probs_ref, values_ref,
    context_hbm, keep_ref, context_ref, sem,
):
    t_rows, width = context_ref.shape
    row = lax.broadcasted_iota(jnp.int32, (t_rows, HEAD_DIM), 0)
    valid = row.astype(jnp.float32) < length_ref[0:1, 0:1]
    for h in range(0, width, HEAD_DIM):
        cols = slice(h, h + HEAD_DIM)
        head = h // HEAD_DIM
        probs_low = probs_ref[:, head * t_rows:(head + 1) * t_rows]
        context = dot(probs_low, values_ref[:, cols], TN)
        context_ref[:, cols] = jnp.where(valid, context, 0.0).astype(jnp.bfloat16)
    out = pltpu.make_async_copy(context_ref, context_hbm, sem)
    out.start()
    half_grad(order, core_ref[0], wk_ref, wv_ref, kg_ref, vg_ref, keep_ref)
    out.wait()


def on_device(memory, key_weight, value_weight, queries, cotangent, target_lengths):
    n_z, n_x = lax.axis_size("z"), lax.axis_size("xh") * lax.axis_size("xl")
    rows, blk = memory.shape[1:]
    t_rows, width = queries.shape[2:]
    depth = key_weight.shape[1]
    n_y = lax.axis_size("y")
    swap = [(0, 1), (1, 0)]
    half = (n_x, n_z, blk, rows)
    core = lax.axis_index("c").reshape(1)
    w_key = key_weight[0]
    w_value, query, cot = (
        pltpu.with_memory_space_constraint(a, pltpu.HBM)
        for a in (value_weight[0], queries[0, 0], cotangent[0, 0])
    )
    vmem = pl.BlockSpec(memory_space=pltpu.VMEM)
    smem = pl.BlockSpec(memory_space=pltpu.SMEM)
    hbm = pl.BlockSpec(memory_space=pltpu.HBM)
    params = pltpu.CompilerParams(vmem_limit_bytes=16 << 20)

    def low(*shape):
        return jax.ShapeDtypeStruct(shape, jnp.bfloat16)

    order = from_member(n_z, n_z * 11 // 16), from_member(n_x, 0)
    sum_order = from_member(n_z, n_z // 2 + 1), from_member(n_x, n_x // 2)
    to_z = jnp.broadcast_to(memory[0].T, (n_z, blk, rows))
    along_z = lax.all_to_all(to_z, "z", 0, 0, axis_index_groups=[order[0]])
    length = jnp.broadcast_to(target_lengths.astype(jnp.float32), (blk, rows))
    tokens = length + lax.ppermute(length, "y", [(y, y ^ 1) for y in range(n_y)])
    along_z, tokens = lax.optimization_barrier((along_z, tokens))
    along_z = along_z.reshape(n_z * blk, rows)
    to_x = jnp.broadcast_to(along_z, (n_x, n_z * blk, rows))
    own = lax.all_to_all(to_x, X, 0, 0, axis_index_groups=[order[1]])
    tokens = tokens + lax.ppermute(tokens, "y", [(y, n_y - 1 - y) for y in range(n_y)])
    own, loss_weight = lax.optimization_barrier((own, float(n_y * t_rows) / tokens))
    other = lax.ppermute(own, "c", swap).reshape(half)
    w_value, query, cot, own_m, key_part = pl.pallas_call(
        functools.partial(own_kernel, order),
        out_shape=(
            low(depth, width), low(t_rows, width), low(t_rows, width), low(rows, depth // 2),
            jax.ShapeDtypeStruct((rows, width), jnp.float32),
        ),
        in_specs=[smem, vmem, vmem, hbm, hbm, hbm],
        out_specs=(vmem,) * 5,
        scratch_shapes=[pltpu.SemaphoreType.DMA((3,))],
        compiler_params=params,
        cost_estimate=pl.CostEstimate(flops=270000000, bytes_accessed=8 << 20, transcendentals=0),
    )(core, own.reshape(half), w_key, w_value, query, cot)
    wide = low(rows, width // HEAD_DIM * t_rows)
    send, key_grad, value_grad, probs, values = pl.pallas_call(
        functools.partial(main_kernel, order, sum_order),
        out_shape=(low(*half), low(rows, width), low(rows, width), wide, low(rows, width)),
        in_specs=[smem] + [vmem] * 8,
        out_specs=(vmem,) * 5,
        compiler_params=params,
        cost_estimate=pl.CostEstimate(flops=1600000000, bytes_accessed=8 << 20, transcendentals=1 << 17),
    )(core, length, other, own_m, key_part, w_key, w_value, query, cot)
    got = lax.ppermute(send, "c", swap)
    context, keep = pl.pallas_call(
        functools.partial(keep_kernel, sum_order),
        out_shape=(low(t_rows, width), low(*half)),
        in_specs=[smem] + [vmem] * 7,
        out_specs=(hbm, vmem),
        scratch_shapes=[pltpu.VMEM((t_rows, width), jnp.bfloat16), pltpu.SemaphoreType.DMA],
        compiler_params=params,
        cost_estimate=pl.CostEstimate(flops=600000000, bytes_accessed=5 << 20, transcendentals=0),
    )(core, length, w_key, w_value, key_grad, value_grad, probs, values)
    pair = (keep.astype(jnp.float32) + got.astype(jnp.float32)).astype(jnp.bfloat16)
    parts = lax.all_to_all(
        pair.reshape(n_x, n_z * blk, rows), X, 0, 0, axis_index_groups=[sum_order[1]]
    )
    row_sum = jnp.sum(parts.astype(jnp.float32), axis=0).astype(jnp.bfloat16)
    parts = lax.all_to_all(row_sum.reshape(n_z, blk, rows), "z", 0, 0, axis_index_groups=[sum_order[0]])
    own_grad = jnp.sum(parts.astype(jnp.float32), axis=0) * loss_weight
    return context[None, None], own_grad.T[None]


def solution(mesh):
    fine = Mesh(mesh.devices.reshape(16, 2, 4, 2, 2), ("z", "xh", "y", "xl", "c"))
    layers, heads, features = ("z", "xh"), ("xl", "c"), ("z", "xh", "xl", "c")
    return jax.shard_map(
        on_device,
        mesh=fine,
        in_specs=(
            P("y", None, features),
            P(layers, None, heads),
            P(layers, None, heads),
            P(layers, "y", None, heads),
            P(layers, "y", None, heads),
            P("y"),
        ),
        out_specs=(P(layers, "y", None, heads), P("y", None, features)),
        check_vma=False,
    )
```
